32 devices in a mesh: head: 4 (over x, core), blk: 8 (over z, y).
Axes of the slice: x: 2, y: 2, z: 4, core: 2. Of those that a mesh axis runs over, the one named last changes fastest.
Arguments:
- query: bfloat16 [4096, 32, 128], P(('blk', 'head')), may hold values from -12 to 12
- keys: bfloat16 [4096, 4, 128], P(('blk', 'head')), may hold values from -12 to 12
- values: bfloat16 [4096, 4, 128], P(('blk', 'head')), may hold values from -6 to 6
- output: bfloat16 [4096, 32, 128], P(('blk', 'head')), may hold values from -1.5 to 1.5
- dout: bfloat16 [4096, 32, 128], P(('blk', 'head')), may hold values from -192 to 192
Outputs:
- dquery: bfloat16 [4096, 32, 128], P(('blk', 'head'))
- dkeys: bfloat16 [4096, 4, 128], P(('blk', 'head'))
- dvalues: bfloat16 [4096, 4, 128], P(('blk', 'head'))
The draws below stay inside these ranges and needn't reach their ends.
All inputs are finite; a program needn't handle non-finite values.
Results may differ from the reference program's by a relative error of at most 0.01.
Values may be sent and summed in bfloat16 or wider, within the bound.
No kernel may reach another device: no remote copies, remote signals or barrier semaphores. Data moves between devices by JAX's collectives and lax.ppermute only.
A program may use at most 192 MiB of HBM per device.

```python
import jax
import jax.numpy as jnp
from jax import lax

HEAD_SIZE = 128
QUERY_HEADS = 32
KEY_VALUE_HEADS = 4
BLOCK_TOKENS = 512
SEQUENCE_TOKENS = 4096
REACH = 1
N_BLK = 8


def draw_query(key, part):
    normalized_rows = jax.random.normal(jax.random.fold_in(key, 11), (SEQUENCE_TOKENS, QUERY_HEADS, HEAD_SIZE), jnp.float32)
    normalized_rows = jnp.clip(normalized_rows, -12.0, 12.0)
    return normalized_rows.astype(jnp.bfloat16)


def draw_keys(key, part):
    normalized_rows = jax.random.normal(jax.random.fold_in(key, 21), (SEQUENCE_TOKENS, KEY_VALUE_HEADS, HEAD_SIZE), jnp.float32)
    normalized_rows = jnp.clip(normalized_rows, -12.0, 12.0)
    return normalized_rows.astype(jnp.bfloat16)


def block_levels(key, dims, cuts, low, top_value):
    loudness, own = 1.0, jax.random.fold_in(key, 6)
    for axis_at, parts in cuts:
        draws = jnp.exp(jax.random.uniform(jax.random.fold_in(own, axis_at), (parts,), jnp.float32, low / len(cuts), top_value / len(cuts)))
        loudness = loudness * jnp.repeat(draws, dims[axis_at] // parts).reshape([-1 if axis == axis_at else 1 for axis in range(len(dims))])
    return loudness


def bell_draw(key, shape, deviation, limit, cuts=(), kind=jnp.bfloat16):
    result = jax.random.normal(key, shape, jnp.float32) * deviation
    if len(cuts) > 0:
        result = block_levels(key, shape, cuts, -0.22, 0.18) * result
    return jnp.clip(result, min=-limit, max=limit).astype(kind)


def setup_inputs(seed: int = 0) -> dict:
    key_of = jax.random.split(jax.random.key(seed), 6)
    return {
        "query": draw_query(jax.random.fold_in(key_of[5], 71), 0),
        "keys": draw_keys(jax.random.fold_in(key_of[5], 71), 0),
        "values": bell_draw(key_of[2], (SEQUENCE_TOKENS, KEY_VALUE_HEADS, HEAD_SIZE), 1.0, 6.0, ((0, 32),)),
        "output": bell_draw(key_of[3], (SEQUENCE_TOKENS, QUERY_HEADS, HEAD_SIZE), 0.25, 1.5, ((0, 32),)),
        "dout": bell_draw(key_of[4], (SEQUENCE_TOKENS, QUERY_HEADS, HEAD_SIZE), 32.0, 192.0, ((0, 32),)),
    }


def head_grads(items):
    query_rows, dout_rows, output_rows, key_rows, value_rows, living_mask = items
    scaling = HEAD_SIZE ** -0.5
    scores = jnp.einsum("qgd,kd->gqk", query_rows, key_rows) * scaling
    scores = jnp.where(living_mask[None, None, :], scores, -jnp.inf)
    row_max = jnp.max(scores, axis=-1, keepdims=True)
    logarithm_sum = row_max + jnp.log(jnp.sum(jnp.exp(scores - row_max), axis=-1, keepdims=True))
    probability_rows = jnp.exp(scores - logarithm_sum)
    probs_low = lax.optimization_barrier(probability_rows.astype(jnp.bfloat16)).astype(jnp.float32)
    delta_rows = jnp.sum(dout_rows * output_rows, axis=-1)
    delta_rows = lax.optimization_barrier(delta_rows.astype(jnp.bfloat16)).astype(jnp.float32)
    delta_rows = jnp.transpose(delta_rows, (1, 0))
    value_grad = jnp.einsum("gqk,qgd->kd", probs_low, dout_rows)
    prob_grad = jnp.einsum("qgd,kd->gqk", dout_rows, value_rows)
    score_grad = probability_rows * (prob_grad - delta_rows[:, :, None]) * scaling
    score_low = lax.optimization_barrier(score_grad.astype(jnp.bfloat16)).astype(jnp.float32)
    query_grad = jnp.einsum("gqk,kd->qgd", score_low, key_rows)
    key_grad = jnp.einsum("gqk,qgd->kd", score_low, query_rows)
    return query_grad.astype(jnp.bfloat16), key_grad, value_grad


def reference(query, keys, values, output, dout):
    query_group_count = QUERY_HEADS // KEY_VALUE_HEADS
    padding_amount = REACH * BLOCK_TOKENS
    neighbour_window = (2 * REACH + 1) * BLOCK_TOKENS
    key_pad = jnp.pad(keys.astype(jnp.float32), ((padding_amount, padding_amount), (0, 0), (0, 0)))
    value_pad = jnp.pad(values.astype(jnp.float32), ((padding_amount, padding_amount), (0, 0), (0, 0)))
    offsets = jnp.arange(neighbour_window, dtype=jnp.int32) // BLOCK_TOKENS - REACH

    def block_step(carry, index):
        key_acc, value_acc = carry
        start = (index * BLOCK_TOKENS).astype(jnp.int32)

        def grouped(array):
            block_portion = lax.dynamic_slice_in_dim(array, start, BLOCK_TOKENS, 0).astype(jnp.float32)
            return jnp.transpose(block_portion.reshape(BLOCK_TOKENS, KEY_VALUE_HEADS, query_group_count, HEAD_SIZE), (1, 0, 2, 3))

        key_rows = jnp.transpose(lax.dynamic_slice_in_dim(key_pad, start, neighbour_window, 0), (1, 0, 2))
        value_rows = jnp.transpose(lax.dynamic_slice_in_dim(value_pad, start, neighbour_window, 0), (1, 0, 2))
        neighbour = index + offsets
        living_mask = (neighbour >= 0) & (neighbour < N_BLK)
        living_heads = jnp.broadcast_to(living_mask[None, :], (KEY_VALUE_HEADS, neighbour_window))
        query_grad, key_grad, value_grad = lax.map(
            head_grads, (grouped(query), grouped(dout), grouped(output), key_rows, value_rows, living_heads))
        query_grad = jnp.transpose(query_grad, (1, 0, 2, 3)).reshape(BLOCK_TOKENS, QUERY_HEADS, HEAD_SIZE)
        key_grad = jnp.transpose(key_grad, (1, 0, 2))
        value_grad = jnp.transpose(value_grad, (1, 0, 2))
        key_acc = lax.dynamic_update_slice_in_dim(
            key_acc, lax.dynamic_slice_in_dim(key_acc, start, neighbour_window, 0) + key_grad, start, 0)
        value_acc = lax.dynamic_update_slice_in_dim(
            value_acc, lax.dynamic_slice_in_dim(value_acc, start, neighbour_window, 0) + value_grad, start, 0)
        return (key_acc, value_acc), query_grad

    zeroed_accumulator = jnp.zeros((SEQUENCE_TOKENS + 2 * padding_amount, KEY_VALUE_HEADS, HEAD_SIZE), jnp.float32)
    indices = jnp.arange(N_BLK, dtype=jnp.int32)
    (key_acc, value_acc), query_grad = lax.scan(block_step, (zeroed_accumulator, zeroed_accumulator), indices)
    dquery = query_grad.reshape(SEQUENCE_TOKENS, QUERY_HEADS, HEAD_SIZE)
    dkeys = key_acc[padding_amount:padding_amount + SEQUENCE_TOKENS].astype(jnp.bfloat16)
    dvalues = value_acc[padding_amount:padding_amount + SEQUENCE_TOKENS].astype(jnp.bfloat16)
    return dquery, dkeys, dvalues
```

```python
import functools
import math

import jax
import jax.numpy as jnp
from jax import lax
from jax.experimental import pallas as pl
from jax.experimental.pallas import tpu as pltpu
from jax.sharding import PartitionSpec as P

F32 = jnp.float32
BF16 = jnp.bfloat16
CORES = 2


def params(n):
    return pltpu.CompilerParams(
        dimension_semantics=("arbitrary",) * n, vmem_limit_bytes=56 * 1024 * 1024
    )


def cost(flops, bytes_, trans=0):
    return pl.CostEstimate(flops=flops, bytes_accessed=bytes_, transcendentals=trans)


def pack_kernel(group, q_ref, do_ref, out_ref, qd_ref, a_scr, b_scr):
    tokens, width = q_ref.shape[0], q_ref.shape[2]
    rows = tokens * group
    a_scr[...] = q_ref[...].astype(F32).reshape(rows, width)
    for j in range(group):
        qd_ref[0, j] = a_scr[pl.ds(j, tokens, stride=group), :].astype(BF16)
    a_scr[...] = do_ref[...].astype(F32).reshape(rows, width)
    b_scr[...] = out_ref[...].astype(F32).reshape(rows, width)
    deltas = []
    for j in range(group):
        d = a_scr[pl.ds(j, tokens, stride=group), :]
        o = b_scr[pl.ds(j, tokens, stride=group), :]
        qd_ref[0, group + j] = d.astype(BF16)
        deltas.append(jnp.sum(jnp.transpose(d * o), axis=0, keepdims=True))
    deltas.append(jnp.zeros((tokens - group, width), F32))
    qd_ref[0, 2 * group] = jnp.concatenate(deltas, axis=0).astype(BF16)


def pack(query, dout, output, group):
    tokens, heads, width = query.shape
    groups = heads // group
    spec = pl.BlockSpec((tokens, group, width), lambda g: (0, g, 0))
    return pl.pallas_call(
        functools.partial(pack_kernel, group),
        grid=(groups,),
        in_specs=[spec] * 3,
        out_specs=pl.BlockSpec((1, 2 * group + 1, tokens, width), lambda g: (g, 0, 0, 0)),
        out_shape=jax.ShapeDtypeStruct((groups, 2 * group + 1, tokens, width), BF16),
        scratch_shapes=[pltpu.VMEM((tokens * group, width), F32)] * 2,
        compiler_params=params(1),
        cost_estimate=cost(4 * query.size, 10 * query.size),
        name="pack",
    )(query, dout, output)


def by_head(sources, f_scr, h_scr):
    groups, keys, width = h_scr.shape
    tokens = keys // len(sources)
    for s, ref in enumerate(sources):
        f_scr[...] = ref[...].astype(F32).reshape(tokens * groups, width)
        for g in range(groups):
            h_scr[g, pl.ds(s * tokens, tokens), :] = f_scr[
                pl.ds(g, tokens, stride=groups), :
            ].astype(BF16)


NT = (((1,), (1,)), ((), ()))
NN = (((1,), (0,)), ((), ()))
TN = (((0,), (0,)), ((), ()))


def dot(a, b, dims):
    return lax.dot_general(a, b, dims, preferred_element_type=F32)


def score_kernel(nx, group, first, coef, *refs):
    valid_ref, refs = refs[0], refs[1:]
    k_refs, refs = refs[:nx], refs[nx:]
    q_refs, refs = refs[:CORES], refs[CORES:]
    if not first:
        (run_ref,), refs = refs[:1], refs[1:]
    p_ref, m_ref, new_ref, f_scr, k_scr = refs
    g = pl.program_id(0)

    @pl.when(g == 0)
    def _():
        by_head(k_refs, f_scr, k_scr)

    k = k_scr[g]
    alive = valid_ref[0] > 0
    for s in range(CORES):
        q = q_refs[s][0].reshape(-1, k.shape[1])
        t = dot(k, q, NT) * coef
        m = jnp.max(t, axis=0, keepdims=True)
        p = jnp.exp2(t - m)
        total = jnp.sum(p, axis=0, keepdims=True)
        p_ref[s, 0] = p.astype(BF16)
        m = jnp.where(alive, m, -jnp.inf)
        m_ref[s, 0] = m
        if first:
            new_ref[s, 0, 0:1] = m
            new_ref[s, 0, 1:2] = total
        else:
            old_m, old_l = run_ref[s, 0, 0:1], run_ref[s, 0, 1:2]
            top = jnp.maximum(old_m, m)
            new_ref[s, 0, 0:1] = top
            new_ref[s, 0, 1:2] = old_l * jnp.exp2(old_m - top) + total * jnp.exp2(m - top)


def scores(valid, k_list, qd_list, run, group):
    groups, _, tokens, width = qd_list[0].shape
    nx = len(k_list)
    keys, rows = tokens * nx, group * tokens
    coef = width ** (-0.5) * math.log2(math.e)
    whole = pl.BlockSpec(k_list[0].shape, lambda g: (0, 0, 0))
    stat = lambda n: pl.BlockSpec((CORES, 1, n, rows), lambda g: (0, g, 0, 0))
    stat_shape = lambda n: jax.ShapeDtypeStruct((CORES, groups, n, rows), F32)
    first = run is None
    return pl.pallas_call(
        functools.partial(score_kernel, nx, group, first, coef),
        grid=(groups,),
        in_specs=[pl.BlockSpec(memory_space=pltpu.SMEM)]
        + [whole] * nx
        + [pl.BlockSpec((1, group, tokens, width), lambda g: (g, 0, 0, 0))] * CORES
        + ([] if first else [stat(2)]),
        out_specs=[
            pl.BlockSpec((CORES, 1, keys, rows), lambda g: (0, g, 0, 0)),
            stat(1),
            stat(2),
        ],
        out_shape=[
            jax.ShapeDtypeStruct((CORES, groups, keys, rows), BF16),
            stat_shape(1),
            stat_shape(2),
        ],
        scratch_shapes=[
            pltpu.VMEM((tokens * groups, width), F32),
            pltpu.VMEM((groups, keys, width), BF16),
        ],
        compiler_params=params(1),
        cost_estimate=cost(
            2 * CORES * groups * keys * rows * width,
            2 * CORES * groups * (keys + width) * rows,
            CORES * groups * keys * rows,
        ),
        name="scores",
    )(valid, *k_list, *qd_list, *([] if first else [run]))


def grad_kernel(nx, group, first, last, scaling, *refs):
    k_refs, refs = refs[:nx], refs[nx:]
    v_refs, refs = refs[:nx], refs[nx:]
    qd_refs, refs = refs[:CORES], refs[CORES:]
    p_ref, m_ref, run_ref, peer_ref, refs = refs[0], refs[1], refs[2], refs[3], refs[4:]
    if not first:
        acc_refs, refs = refs[:CORES], refs[CORES:]
    d_refs, refs = refs[:nx], refs[nx:]
    dq_refs, refs = refs[:CORES], refs[CORES:]
    f_scr, k_scr, v_scr = refs
    g = pl.program_id(0)

    @pl.when(g == 0)
    def _():
        by_head(k_refs, f_scr, k_scr)
        by_head(v_refs, f_scr, v_scr)

    k, v = k_scr[g], v_scr[g]
    width = k.shape[1]
    dk = dv = None
    for s in range(CORES):
        q = qd_refs[s][0, :group].reshape(-1, width)
        do = qd_refs[s][0, group : 2 * group].reshape(-1, width)
        packed = qd_refs[s][0, 2 * group].astype(F32)
        delta = jnp.concatenate([packed[j : j + 1] for j in range(group)], axis=1)
        m_a, l_a = run_ref[s, 0, 0:1], run_ref[s, 0, 1:2]
        m_b, l_b = peer_ref[1 - s, 0, 0:1], peer_ref[1 - s, 0, 1:2]
        top = jnp.maximum(m_a, m_b)
        total = l_a * jnp.exp2(m_a - top) + l_b * jnp.exp2(m_b - top)
        factor = jnp.exp2(m_ref[s, 0] - top) / total
        prob = p_ref[s, 0].astype(F32) * factor
        dp = dot(v, do, NT)
        ds = (prob * (dp - delta)).astype(BF16)
        dv_s = dot(prob.astype(BF16), do, NN)
        dk_s = dot(ds, q, NN)
        dv = dv_s if dv is None else dv + dv_s
        dk = dk_s if dk is None else dk + dk_s
        dq = dot(ds, k, TN)
        if not first:
            dq = dq + acc_refs[s][0]
        if last:
            dq = dq * scaling
        dq_refs[s][0] = dq.astype(dq_refs[s].dtype)
    dk = dk * scaling
    tokens = dk.shape[0] // nx
    for i in range(nx):
        d_refs[i][0, 0] = dk[i * tokens : (i + 1) * tokens].astype(d_refs[i].dtype)
        d_refs[i][1, 0] = dv[i * tokens : (i + 1) * tokens].astype(d_refs[i].dtype)


def grads(k_list, v_list, qd_list, p, m, run, peer, acc, group, last):
    groups, _, tokens, width = qd_list[0].shape
    nx = len(k_list)
    keys, rows = tokens * nx, group * tokens
    first = acc is None
    whole = pl.BlockSpec(k_list[0].shape, lambda g: (0, 0, 0))
    stat = lambda n: pl.BlockSpec((CORES, 1, n, rows), lambda g: (0, g, 0, 0))
    row = pl.BlockSpec((1, rows, width), lambda g: (g, 0, 0))
    d_types = [F32] + [BF16] * (nx - 1)
    q_types = [F32, BF16] if last else [F32, F32]
    out = pl.pallas_call(
        functools.partial(grad_kernel, nx, group, first, last, width ** (-0.5)),
        grid=(groups,),
        in_specs=[whole] * (2 * nx)
        + [pl.BlockSpec((1, 2 * group + 1, tokens, width), lambda g: (g, 0, 0, 0))] * CORES
        + [pl.BlockSpec((CORES, 1, keys, rows), lambda g: (0, g, 0, 0)), stat(1), stat(2), stat(2)]
        + ([] if first else [row] * CORES),
        out_specs=[pl.BlockSpec((2, 1, tokens, width), lambda g: (0, g, 0, 0))] * nx + [row] * CORES,
        out_shape=[jax.ShapeDtypeStruct((2, groups, tokens, width), t) for t in d_types]
        + [jax.ShapeDtypeStruct((groups, rows, width), t) for t in q_types],
        scratch_shapes=[
            pltpu.VMEM((tokens * groups, width), F32),
            pltpu.VMEM((groups, keys, width), BF16),
            pltpu.VMEM((groups, keys, width), BF16),
        ],
        compiler_params=params(1),
        cost_estimate=cost(
            8 * CORES * groups * keys * rows * width,
            CORES * groups * (2 * keys + 12 * width) * rows,
        ),
        name="grads",
    )(*k_list, *v_list, *qd_list, p, m, run, peer, *([] if first else acc))
    return list(out[:nx]), list(out[nx:])


def finish_kernel(group, count, *refs):
    out_ref, scr = refs[-2], refs[-1]
    tokens = out_ref.shape[0]
    for j in range(group):
        total = refs[0][0, j].astype(F32)
        for ref in refs[1:count]:
            total = total + ref[0, j].astype(F32)
        scr[pl.ds(j, tokens, stride=group), :] = total
    out_ref[...] = scr[...].reshape(tokens, group, -1).astype(out_ref.dtype)


def finish(terms, plane, group):
    groups = terms[0].shape[1] // group
    tokens, width = terms[0].shape[2:]
    return pl.pallas_call(
        functools.partial(finish_kernel, group, len(terms)),
        grid=(groups,),
        in_specs=[pl.BlockSpec((1, group, tokens, width), lambda g: (plane, g, 0, 0))] * len(terms),
        out_specs=pl.BlockSpec((tokens, group, width), lambda g: (0, g, 0)),
        out_shape=jax.ShapeDtypeStruct((tokens, groups * group, width), BF16),
        scratch_shapes=[pltpu.VMEM((tokens * group, width), F32)],
        compiler_params=params(1),
        cost_estimate=cost(terms[0].size, 4 * terms[0].size),
        name="finish",
    )(*terms)


def shifted(value, axis, by):
    size = lax.axis_size(axis)
    pairs = [(i, i + by) for i in range(size) if 0 <= i + by < size]
    return lax.ppermute(value, axis, pairs)


def rotated(value, by):
    size = lax.axis_size("head")
    return lax.ppermute(value, "head", [(i, (i + by) % size) for i in range(size)])


def other_core(value):
    size = lax.axis_size("head")
    return lax.ppermute(value, "head", [(i, i ^ 1) for i in range(size)])


def on_device(query, keys, values, output, dout):
    blocks = lax.axis_size("blk")
    reach = blocks // 8
    position = lax.axis_index("blk")
    columns = lax.axis_size("head") // CORES
    heads, width = query.shape[1:]
    kv_heads = keys.shape[1]
    group = heads // kv_heads
    tokens = query.shape[0]

    def gathered(value):
        return [value] + [rotated(value, CORES * s) for s in range(1, columns)]

    raw = {}
    for name, value in (("k", keys), ("v", values)):
        for direction in (1, -1):
            moving = value
            for distance in range(1, reach + 1):
                moving = shifted(moving, "blk", direction)
                raw[name, direction, distance] = moving
    qd_mine = pack(query, dout, output, group)
    qd = [qd_mine, other_core(qd_mine)]

    places = [(0, 0)] + [(d, n) for n in range(1, reach + 1) for d in (1, -1)]
    rows_k, rows_v, probs, tops = {}, {}, {}, {}
    run = None
    for place in places:
        rows_k[place] = gathered(raw[("k",) + place] if place[1] else keys)
        source = position - place[0] * place[1]
        valid = ((source >= 0) & (source < blocks)).astype(jnp.int32).reshape(1)
        probs[place], tops[place], run = scores(valid, rows_k[place], qd, run, group)
    for place in places:
        rows_v[place] = gathered(raw[("v",) + place] if place[1] else values)
    peer = other_core(run)

    acc = None

    def block_grads(place, last=False):
        nonlocal acc
        parts, acc = grads(
            rows_k[place], rows_v[place], qd, probs[place], tops[place], run, peer, acc, group, last
        )
        return [parts[0]] + [rotated(parts[s], -CORES * s) for s in range(1, columns)]

    def summed(terms):
        total = terms[0].astype(F32)
        for term in terms[1:]:
            total = total + term.astype(F32)
        return total

    arrived = []
    for direction in (1, -1):
        carried = []
        for distance in range(reach, 0, -1):
            total = summed(block_grads((direction, distance)) + carried)
            carried = [shifted(total.astype(BF16), "blk", -direction)]
        arrived += carried
    own = block_grads((0, 0), last=True) + arrived
    by_rows = lambda x: x.reshape(1, heads, tokens, width)
    dquery = finish([by_rows(acc[0]), by_rows(other_core(acc[1]))], 0, group)
    return dquery, finish(own, 0, kv_heads), finish(own, 1, kv_heads)


def solution(mesh):
    spec = P(("blk", "head"), None, None)
    return jax.shard_map(
        on_device, mesh=mesh, in_specs=(spec,) * 5, out_specs=(spec,) * 3, check_vma=False
    )
```

```python
import functools
import math

import jax
import jax.numpy as jnp
from jax import lax
from jax.experimental import pallas as pl
from jax.experimental.pallas import tpu as pltpu
from jax.sharding import PartitionSpec as P


F32 = jnp.float32
BF16 = jnp.bfloat16
CORES = 2
VMEM = pl.BlockSpec(memory_space=pltpu.VMEM)
HBM = pl.BlockSpec(memory_space=pltpu.HBM)
SMEM = pl.BlockSpec(memory_space=pltpu.SMEM)
NT = (((1,), (1,)), ((), ()))
NN = (((1,), (0,)), ((), ()))
TN = (((0,), (0,)), ((), ()))


def dot(a, b, dims):
    return lax.dot_general(a, b, dims, preferred_element_type=F32)


def call(kernel, in_specs, out_shapes, scratch, flops, limit, *args):
    outs = [s if isinstance(s, jax.ShapeDtypeStruct) else jax.ShapeDtypeStruct(*s) for s in out_shapes]
    total = sum(math.prod(x.shape) * x.dtype.itemsize for x in [*args, *outs])
    return pl.pallas_call(
        kernel,
        in_specs=in_specs,
        out_specs=[VMEM] * len(outs),
        out_shape=outs,
        scratch_shapes=scratch,
        compiler_params=pltpu.CompilerParams(vmem_limit_bytes=limit * 1024 * 1024),
        cost_estimate=pl.CostEstimate(flops=flops, bytes_accessed=total, transcendentals=0),
    )(*args)


def pack_kernel(group, q_ref, do_ref, out_ref, qd_ref, in_scr, a_scr, b_scr, sems):
    groups, _, tokens, width = qd_ref.shape
    rows = tokens * group
    sources = (q_ref, do_ref, out_ref)

    def copy(g, i):
        heads = pl.ds(g * group, group)
        return pltpu.make_async_copy(sources[i].at[:, heads, :], in_scr.at[g, i], sems.at[g, i])

    for g in range(groups):
        for i in range(len(sources)):
            copy(g, i).start()
    for g in range(groups):
        copy(g, 0).wait()
        a_scr[...] = in_scr[g, 0].astype(F32).reshape(rows, width)
        for j in range(group):
            qd_ref[g, j] = a_scr[pl.ds(j, tokens, stride=group), :].astype(BF16)
        copy(g, 1).wait()
        copy(g, 2).wait()
        a_scr[...] = in_scr[g, 1].astype(F32).reshape(rows, width)
        b_scr[...] = in_scr[g, 2].astype(F32).reshape(rows, width)
        deltas = []
        for j in range(group):
            d = a_scr[pl.ds(j, tokens, stride=group), :]
            o = b_scr[pl.ds(j, tokens, stride=group), :]
            qd_ref[g, group + j] = d.astype(BF16)
            deltas.append(jnp.sum(jnp.transpose(d * o), axis=0, keepdims=True))
        deltas.append(jnp.zeros((tokens - group, width), F32))
        qd_ref[g, 2 * group] = jnp.concatenate(deltas, axis=0).astype(BF16)


def pack(query, dout, output, group):
    tokens, heads, width = query.shape
    groups = heads // group
    shape = (groups, 2 * group + 1, tokens, width)
    return call(
        functools.partial(pack_kernel, group), [HBM] * 3, [(shape, BF16)],
        [pltpu.VMEM((groups, 3, tokens, group, width), BF16)]
        + [pltpu.VMEM((tokens * group, width), F32)] * 2
        + [pltpu.SemaphoreType.DMA((groups, 3))],
        4 * query.size, 59, query, dout, output,
    )[0]


def by_head(sources, f_scr, h_scr):
    groups, keys, width = h_scr.shape
    tokens = keys // len(sources)
    for s, ref in enumerate(sources):
        f_scr[...] = ref[...].astype(F32).reshape(tokens * groups, width)
        for g in range(groups):
            h_scr[g, pl.ds(s * tokens, tokens), :] = f_scr[
                pl.ds(g, tokens, stride=groups), :
            ].astype(BF16)


def score_kernel(nx, group, first, scaling, *refs):
    valid_ref, refs = refs[0], refs[1:]
    k_refs, refs = refs[:nx], refs[nx:]
    q_refs, refs = refs[:CORES], refs[CORES:]
    if not first:
        (run_ref,), refs = refs[:1], refs[1:]
    p_ref, m_ref, new_ref, f_scr, k_scr = refs
    by_head(k_refs, f_scr, k_scr)
    groups, keys, width = k_scr.shape
    tokens = keys // nx
    alive = valid_ref[0] > 0
    two = 2 * tokens

    def body(g, _):
        for s in range(CORES):
            for j in range(0, group, 2):
                q = q_refs[s][g, j : j + 2].reshape(two, width)
                cols = pl.ds(j * tokens, two)
                tops, sums = [], []
                for x in range(nx):
                    part = pl.ds(x * tokens, tokens)
                    t = dot(k_scr[g, part, :], q, NT)
                    m = jnp.max(t, axis=0, keepdims=True)
                    p = jnp.exp((t - m) * scaling)
                    p_ref[s, g, part, cols] = p.astype(BF16)
                    m = jnp.where(alive, m * scaling, -jnp.inf)
                    m_ref[s, g, x : x + 1, cols] = m
                    tops.append(m)
                    sums.append(jnp.sum(p, axis=0, keepdims=True))
                if first:
                    top, total = tops.pop(0), sums.pop(0)
                else:
                    top, total = run_ref[s, g, 0:1, cols], run_ref[s, g, 1:2, cols]
                for m, l in zip(tops, sums):
                    new = jnp.maximum(top, m)
                    total = total * jnp.exp(top - new) + l * jnp.exp(m - new)
                    top = new
                new_ref[s, g, 0:1, cols] = top
                new_ref[s, g, 1:2, cols] = total
        return 0

    lax.fori_loop(0, groups, body, 0)


def scores(valid, k_list, qd_list, run, group):
    groups, _, tokens, width = qd_list[0].shape
    nx = len(k_list)
    keys, rows = tokens * nx, group * tokens
    first = run is None
    args = [valid, *k_list, *qd_list] + ([] if first else [run])
    return call(
        functools.partial(score_kernel, nx, group, first, width ** (-0.5)),
        [SMEM] + [VMEM] * (len(args) - 1),
        [((CORES, groups, keys, rows), BF16), ((CORES, groups, nx, rows), F32), ((CORES, groups, 2, rows), F32)],
        [pltpu.VMEM((tokens * groups, width), F32), pltpu.VMEM((groups, keys, width), BF16)],
        2 * CORES * groups * keys * rows * width, 24, *args,
    )


def grad_kernel(nx, group, first, last, scaling, *refs):
    k_refs, refs = refs[:nx], refs[nx:]
    v_refs, refs = refs[:nx], refs[nx:]
    qd_refs, refs = refs[:CORES], refs[CORES:]
    p_ref, m_ref, run_ref, peer_ref, refs = refs[0], refs[1], refs[2], refs[3], refs[4:]
    if not first:
        acc_refs, refs = refs[:CORES], refs[CORES:]
    d_refs, refs = refs[:nx], refs[nx:]
    dq_refs, refs = refs[:CORES], refs[CORES:]
    f_scr, k_scr, v_scr, p_scr, s_scr = refs
    by_head(k_refs, f_scr, k_scr)
    by_head(v_refs, f_scr, v_scr)
    groups, keys, width = k_scr.shape
    tokens = keys // nx
    rows = group * tokens
    two = 2 * tokens

    def body(g, _):
        for s in range(CORES):
            packed = qd_refs[s][g, 2 * group].astype(F32)
            m_a, l_a = run_ref[s, g, 0:1], run_ref[s, g, 1:2]
            m_b, l_b = peer_ref[1 - s, g, 0:1], peer_ref[1 - s, g, 1:2]
            top = jnp.maximum(m_a, m_b)
            total = l_a * jnp.exp(m_a - top) + l_b * jnp.exp(m_b - top)
            factors = [jnp.exp(m_ref[s, g, x : x + 1] - top) / total for x in range(nx)]
            for j in range(0, group, 2):
                do = qd_refs[s][g, group + j : group + j + 2].reshape(two, width)
                delta = jnp.concatenate([packed[j : j + 1], packed[j + 1 : j + 2]], axis=1)
                lo = j * tokens
                for x in range(nx):
                    part = pl.ds(x * tokens, tokens)
                    prob = p_ref[s, g, part, pl.ds(lo, two)].astype(F32) * factors[x][:, lo : lo + two]
                    p_scr[part, pl.ds(s * rows + lo, two)] = prob.astype(BF16)
                    dp = dot(v_scr[g, part, :], do, NT)
                    s_scr[part, pl.ds(s * rows + lo, two)] = (prob * (dp - delta)).astype(BF16)
                dq = dot(s_scr[:, pl.ds(s * rows + lo, two)], k_scr[g], TN)
                if not first:
                    dq = dq + acc_refs[s][g, pl.ds(lo, two), :]
                if last:
                    dq = dq * scaling
                dq_refs[s][g, pl.ds(lo, two), :] = dq.astype(dq_refs[s].dtype)
        dk = dv = None
        for s in range(CORES):
            cols = pl.ds(s * rows, rows)
            dv_s = dot(p_scr[:, cols], qd_refs[s][g, group : 2 * group].reshape(rows, width), NN)
            dk_s = dot(s_scr[:, cols], qd_refs[s][g, :group].reshape(rows, width), NN)
            dv = dv_s if dv is None else dv + dv_s
            dk = dk_s if dk is None else dk + dk_s
        dk = dk * scaling
        for i in range(nx):
            d_refs[i][0, g] = dk[i * tokens : (i + 1) * tokens].astype(d_refs[i].dtype)
            d_refs[i][1, g] = dv[i * tokens : (i + 1) * tokens].astype(d_refs[i].dtype)
        return 0

    lax.fori_loop(0, groups, body, 0)


def grads(k_list, v_list, qd_list, p, m, run, peer, acc, group, last):
    groups, _, tokens, width = qd_list[0].shape
    nx = len(k_list)
    keys, rows = tokens * nx, group * tokens
    first = acc is None
    args = [*k_list, *v_list, *qd_list, p, m, run, peer] + ([] if first else acc)
    d_types = [F32] + [BF16] * (nx - 1)
    q_types = [F32, BF16] if last else [F32, F32]
    out = call(
        functools.partial(grad_kernel, nx, group, first, last, width ** (-0.5)),
        [VMEM] * len(args),
        [((2, groups, tokens, width), t) for t in d_types] + [((groups, rows, width), t) for t in q_types],
        [
            pltpu.VMEM((tokens * groups, width), F32),
            pltpu.VMEM((groups, keys, width), BF16),
            pltpu.VMEM((groups, keys, width), BF16),
            pltpu.VMEM((keys, CORES * rows), BF16),
            pltpu.VMEM((keys, CORES * rows), BF16),
        ],
        8 * CORES * groups * keys * rows * width, 30, *args,
    )
    return list(out[:nx]), list(out[nx:])


def finish_kernel(group, count, *refs):
    terms, outs, scr = refs[:count], refs[count:-1], refs[-1]
    tokens = outs[0].shape[0]
    for p, out_ref in enumerate(outs):
        for g in range(terms[0].shape[1] // group):
            for j in range(group):
                total = terms[0][p, g * group + j].astype(F32)
                for ref in terms[1:]:
                    total = total + ref[p, g * group + j].astype(F32)
                scr[pl.ds(j, tokens, stride=group), :] = total
            out_ref[:, pl.ds(g * group, group), :] = (
                scr[...].reshape(tokens, group, -1).astype(out_ref.dtype)
            )


def finish(terms, group):
    planes, heads, tokens, width = terms[0].shape
    return call(
        functools.partial(finish_kernel, group, len(terms)), [VMEM] * len(terms),
        [((tokens, heads, width), BF16)] * planes,
        [pltpu.VMEM((tokens * group, width), F32)], terms[0].size, 16, *terms,
    )


def moved(value, ahead, across):
    blocks, size = lax.axis_size("blk"), lax.axis_size("head")
    pairs = [
        (h * blocks + b, (h + CORES * across) % size * blocks + b + ahead)
        for h in range(size)
        for b in range(blocks)
        if 0 <= b + ahead < blocks
    ]
    return lax.ppermute(value, ("head", "blk"), pairs)


def other_core(value):
    size = lax.axis_size("head")
    return lax.ppermute(value, "head", [(i, i ^ 1) for i in range(size)])


def on_device(query, keys, values, output, dout):
    blocks = lax.axis_size("blk")
    reach = blocks // 8
    position = lax.axis_index("blk")
    columns = lax.axis_size("head") // CORES
    heads, width = query.shape[1:]
    kv_heads = keys.shape[1]
    group = heads // kv_heads
    tokens = query.shape[0]

    def fetch(value):
        got = {(0, 0): [value] + [moved(value, 0, s) for s in range(1, columns)]}
        for direction in (1, -1):
            moving = value
            for distance in range(1, reach + 1):
                place = (direction, distance)
                here = moved(moving, direction, 0)
                others = [moved(moving, direction, s) for s in range(1, columns)]
                got[place] = [here] + others
                moving = here
        return got

    rows_k, rows_v = fetch(keys), fetch(values)
    qd_mine = pack(query, dout, output, group)
    qd = [qd_mine, other_core(qd_mine)]

    places = [(0, 0)] + [(d, n) for n in range(1, reach + 1) for d in (1, -1)]
    probs, tops = {}, {}
    run = None
    for place in places:
        source = position - place[0] * place[1]
        valid = ((source >= 0) & (source < blocks)).astype(jnp.int32).reshape(1)
        probs[place], tops[place], run = scores(valid, rows_k[place], qd, run, group)
    peer = other_core(run)

    acc = None

    def block_grads(place, last=False):
        nonlocal acc
        parts, acc = grads(
            rows_k[place], rows_v[place], qd, probs[place], tops[place], run, peer, acc, group, last
        )
        return [parts[0]] + [moved(parts[s], 0, -s) for s in range(1, columns)]

    def summed(terms):
        total = terms[0].astype(F32)
        for term in terms[1:]:
            total = total + term.astype(F32)
        return total

    arrived = []
    for direction in (1, -1):
        carried = []
        for distance in range(reach, 0, -1):
            total = summed(block_grads((direction, distance)) + carried)
            carried = [moved(total.astype(BF16), -direction, 0)]
        arrived += carried
    own = block_grads((0, 0), last=True) + arrived
    by_rows = lambda x: x.reshape(1, heads, tokens, width)
    back = other_core(acc[1])
    dquery = finish([by_rows(acc[0]), by_rows(back)], group)[0]
    dkeys, dvalues = finish(own, kv_heads)
    return dquery, dkeys, dvalues


def solution(mesh):
    spec = P(("blk", "head"), None, None)

    return jax.shard_map(
        on_device, mesh=mesh, in_specs=(spec,) * 5, out_specs=(spec,) * 3, check_vma=False
    )
```
